256 devices in a mesh: rows: 128 (over y, z, x), cols: 2 (over core).
Axes of the slice: x: 4, y: 4, z: 8, core: 2. Of those that a mesh axis runs over, the one named last changes fastest.
Arguments:
- panels: float32 [98304, 2, 768], P('rows', None, 'cols'), as said below
- closure_cols: int32 [1024, 12], P('rows'), may hold values from -1 to 15, as said below
Outputs:
- factor: float32 [98304, 2, 768], P('rows', None, 'cols')
The draws below stay inside these ranges and needn't reach their ends.
Inputs may be any that keep to these rules, and one draw needn't show every extreme that they name: `closure_cols`: each entry is a block column 0 to 15 of the two supernodes or -1 for an empty slot; entries may repeat; the supernodes' own rows are not read. The block (rows 0 to 767 of panel 0) and the 1536 by 1536 matrix formed by it and rows 768 to 1535 of both panels, mirrored, is symmetric positive definite.
All inputs are finite; a program needn't handle non-finite values.
Results may differ from the reference program's by a relative error of at most 0.000092.
Values sent between devices are 32-bit elements; how exact they have to be, the bound alone decides.
No kernel may reach another device: no remote copies, remote signals or barrier semaphores. Data moves between devices by JAX's collectives and lax.ppermute only.
A program may use at most 128 MiB of HBM per device.

```python
import jax
import jax.numpy as jnp
from jax import lax

B = 96
S = 8
K = 12
R = 8
W = 768
NB = 1024


def draw_panels(key, part):
    key_rows = jax.random.fold_in(key, 0)
    key_mix = jax.random.fold_in(key, 2)
    key_diag = jax.random.fold_in(key, 3)
    total_rows = NB * B
    below = jax.random.normal(key_rows, (total_rows, 2, W), jnp.float32)
    mixing = jax.random.normal(key_mix, (2 * W, 2 * W), jnp.float32) / jnp.sqrt(2.0 * W)
    dense = jnp.dot(mixing, mixing.T, precision=lax.Precision.HIGHEST)
    dense = 0.5 * (dense + dense.T)
    extra = jnp.exp(jax.random.uniform(key_diag, (2 * W,), jnp.float32, -0.7, 0.7))
    dense = dense + jnp.diag(extra)
    top_rows = jnp.concatenate([dense[:W, :W], jnp.zeros((W, W), jnp.float32)], axis=1).reshape(W, 2, W)
    low_rows = dense[W:, :].reshape(W, 2, W)
    result = below.at[:W].set(top_rows)
    result = result.at[R * B:R * B + W].set(low_rows)
    return result


def draw_closure_cols(key, part):
    key_count, key_vals = jax.random.split(jax.random.fold_in(key, 7), 2)
    counts = jax.random.randint(key_count, (NB, 1), 2 * K // 3, K + 1)
    values = jax.random.randint(key_vals, (NB, K), 0, 2 * S)
    slots = jnp.arange(K)[None, :]
    result = jnp.where(slots < counts, values, -1)
    full_row = values[NB - 1].at[0].set(2 * S - 1)
    result = result.at[NB - 1].set(full_row)
    result = result.at[NB - 2].set(jnp.full((K,), -1, jnp.int32))
    return result.astype(jnp.int32)


def setup_inputs(seed: int = 0) -> dict:
    arg_keys = jax.random.split(jax.random.key(seed), 3)
    return {
        "panels": draw_panels(jax.random.fold_in(arg_keys[2], 71), 0),
        "closure_cols": draw_closure_cols(jax.random.fold_in(arg_keys[2], 71), 0),
    }


def reference(panels, closure_cols):
    rows_total = panels.shape[0]
    block_count = rows_total // B
    block_ids = jnp.arange(block_count)
    column_ids = jnp.arange(2 * S)
    touched = jnp.any(closure_cols[:, :, None] == column_ids[None, None, :], axis=1)
    in_first = block_ids < S
    in_second = (block_ids >= R) & (block_ids < R + S)
    present = jnp.where(in_first[:, None], column_ids[None, :] < S, jnp.where(in_second[:, None], True, touched))
    present = present.astype(jnp.float32)
    kept = panels.reshape(block_count, B, 2, S, B) * present.reshape(block_count, 1, 2, S, 1)
    kept = kept.reshape(rows_total, 2, W)
    first = kept[:, 0, :]
    second = kept[:, 1, :]
    lead_factor = jnp.linalg.cholesky(first[:W])
    panel_one = lax.linalg.triangular_solve(lead_factor, first, left_side=False, lower=True, transpose_a=True)
    lower_left = panel_one[R * B:R * B + W]
    updated = second - jnp.dot(panel_one, lower_left.T, precision=lax.Precision.HIGHEST)
    tail_factor = jnp.linalg.cholesky(updated[R * B:R * B + W])
    panel_two = lax.linalg.triangular_solve(tail_factor, updated, left_side=False, lower=True, transpose_a=True)
    keep_rows = jnp.repeat(1.0 - in_first.astype(jnp.float32), B)
    panel_two = panel_two * keep_rows[:, None]
    return jnp.stack([panel_one, panel_two], axis=1)
```

```python
import jax
import jax.numpy as jnp
from jax import lax
from jax.experimental import pallas as pl
from jax.experimental.pallas import tpu as pltpu
from jax.sharding import PartitionSpec as P

B = 96
S = 8
R = 8
N = 128
CHIPS = 128
BF = jnp.bfloat16


def split3(x):
    high = x.astype(BF).astype(jnp.float32)
    rest = x - high
    mid = rest.astype(BF).astype(jnp.float32)
    return high, mid, rest - mid


def rows_of(x, k):
    return jnp.broadcast_to(x[k : k + 1, :], (8, N))


def lanes_of(x, k):
    return jnp.broadcast_to(x[:, k : k + 1], (8, N))


def block_kernel(s_ref, o_ref):
    lane = lax.broadcasted_iota(jnp.int32, (8, N), 1)
    sub = lax.broadcasted_iota(jnp.int32, (8, N), 0)
    rows = [s_ref[8 * i : 8 * i + 8, :] for i in range(16)]
    for g in range(16):
        slab, at = rows[g], 8 * g
        inside = (lane >= at) & (lane < at + 8)
        cols = [lanes_of(slab, at + j) for j in range(8)]
        scales = None
        look = g + 1 < 16
        if look:
            following = jnp.where(inside, 0.0, rows[g + 1])
            fcols = [lanes_of(rows[g + 1], at + j) for j in range(8)]
        for k in range(8):
            inv = 1.0 / rows_of(cols[k], k)
            mult = jnp.where(sub > k, cols[k] * inv, 0.0)
            pivot = jnp.where(lane == at + k, 1.0, rows_of(slab, k))
            heads = [rows_of(cols[j], k) for j in range(k + 1, 8)]
            if look:
                fmult = fcols[k] * inv
                following = following - fmult * jnp.where((lane > at + k) & (lane < at + 8), 0.0, pivot)
                for j in range(k + 1, 8):
                    fcols[j] = fcols[j] - fmult * heads[j - k - 1]
            slab = jnp.where((lane == at + k) & (sub > k), 0.0, slab) - mult * pivot
            for j in range(k + 1, 8):
                cols[j] = cols[j] - mult * heads[j - k - 1]
            scales = inv if scales is None else jnp.where(sub == k, inv, scales)
        solved = jnp.where(lane == at + sub, 1.0, jnp.where((lane > at + sub) & (lane < at + 8), 0.0, slab))
        if look:
            rows[g + 1] = following
        if g + 2 < 16:
            a = split3(jnp.where(lane >= at + 16, slab * scales, 0.0))
            b = split3(solved)
            left = jnp.concatenate([a[0], a[0], a[1], a[0], a[2], a[1]], 0).astype(BF)
            right = jnp.concatenate([b[0], b[1], b[0], b[2], b[0], b[1]], 0).astype(BF)
            change = lax.dot_general(left, right, (((0,), (0,)), ((), ())), preferred_element_type=jnp.float32)
            for i in range(g + 2, 16):
                rows[i] = jnp.where(inside, 0.0, rows[i]) - change[8 * i : 8 * i + 8, :]
        o_ref[at : at + 8, :] = jnp.where(lane <= at + sub, solved, 0.0) * jnp.sqrt(scales)


def block_inverse(block):
    return pl.pallas_call(
        block_kernel,
        out_shape=jax.ShapeDtypeStruct((N, N), jnp.float32),
        cost_estimate=pl.CostEstimate(flops=3_000_000_000, bytes_accessed=131072, transcendentals=0),
    )(block)


def outer(left, right):
    return lax.dot_general(
        left, right, (((1,), (1,)), ((), ())), precision=lax.Precision.HIGH, preferred_element_type=jnp.float32
    )


ORDERS = ((0, 2, 5, 1, 6, 3, 4), (2, 5, 0, 3, 4, 1, 6))


def send(piece, pairs_of):
    pairs = []
    for core in range(2):
        pairs += [(2 * a + core, 2 * b + core) for a, b in pairs_of(ORDERS[core])]
    return lax.ppermute(piece, ("rows", "cols"), pairs)


def spread(piece, root, splits, row, core):
    def bit(k):
        return (((row ^ root) >> jnp.where(core == 0, ORDERS[0][k], ORDERS[1][k])) & 1) == 1

    def holders(order, k):
        done = sum(1 << b for b in order[:k])
        return [(i ^ root, i ^ root ^ (1 << order[k])) for i in range(CHIPS) if i & ~done == 0]

    for k in range(7):
        if k < splits:
            half = piece.shape[0] // 2
            got = send(piece[half:], lambda order: holders(order, k))
            piece = jnp.where(bit(k), got, piece[:half])
        else:
            got = send(piece, lambda order: holders(order, k))
            piece = jnp.where(bit(k), got, piece)
    for k in reversed(range(splits)):
        got = send(piece, lambda order: [(i, i ^ (1 << order[k])) for i in range(CHIPS)])
        mine = bit(k)
        piece = jnp.concatenate([jnp.where(mine, got, piece), jnp.where(mine, piece, got)], 0)
    return piece


def whole(half, core):
    other = lax.ppermute(half, "cols", [(0, 1), (1, 0)])
    return jnp.concatenate([jnp.where(core == 0, half, other), jnp.where(core == 0, other, half)], 1)


def factor_panel(top):
    width = top.shape[1]
    inverses, columns = [], []
    for j in range(width // N):
        inverse = block_inverse(top[:N, :N])
        column = outer(top[N:, :N], inverse)
        inverses.append(inverse)
        columns.append(column)
        left = width - N * (j + 1)
        if left:
            top = top[N:, N:] - outer(column, column[:left])
    return inverses, columns


def per_device(panels, closure_cols):
    local_rows = panels.shape[0]
    half_width = panels.shape[2]
    width = 2 * half_width
    block_count = local_rows // B
    row = lax.axis_index("rows")
    core = lax.axis_index("cols")
    first_half = panels[:, 0, :]
    second_half = panels[:, 1, :]

    lead = whole(spread(first_half, 0, 3, row, core), core)
    first = whole(first_half, core)
    second = whole(second_half, core)
    low = spread(jnp.concatenate([first_half, second_half], 0).reshape(4, width // 2, half_width), 1, 2, row, core)
    low = low.reshape(2 * width, half_width)
    low_first = whole(low[:width], core)
    low_second = whole(low[width:], core)

    block_ids = row * block_count + jnp.arange(block_count)
    column_ids = jnp.arange(2 * S)
    touched = jnp.any(closure_cols[:, :, None] == column_ids[None, None, :], axis=1)
    in_first = block_ids < S
    in_second = (block_ids >= R) & (block_ids < R + S)
    present = jnp.where(
        in_first[:, None], column_ids[None, :] < S, jnp.where(in_second[:, None], True, touched)
    )
    mask = jnp.repeat(jnp.repeat(present.astype(jnp.float32), B, axis=0), B, axis=1)
    first = first * mask[:, :width]
    second = second * mask[:, width:]

    inverses, columns = factor_panel(jnp.concatenate([lead, first], 0))
    steps = width // N
    one = [column[-local_rows:] for column in columns]
    solved, rest = [], low_first
    for j in range(steps):
        part = outer(rest[:, :N], inverses[j])
        solved.append(part)
        left = width - N * (j + 1)
        if left:
            rest = rest[:, N:] - outer(part, columns[j][:left])
    lower_left = jnp.concatenate(solved, 1)
    rows = jnp.concatenate([lower_left, jnp.concatenate(one, 1)], 0)
    _, columns = factor_panel(jnp.concatenate([low_second, second], 0) - outer(rows, lower_left))
    keep_rows = jnp.repeat(1.0 - in_first.astype(jnp.float32), B)[:, None]
    two = [column[-local_rows:] * keep_rows for column in columns]

    def own(parts):
        half = steps // 2
        return jnp.concatenate([jnp.where(core == 0, parts[i], parts[i + half]) for i in range(half)], 1)

    return jnp.stack([own(one), own(two)], axis=1)


def solution(mesh):
    in_specs = (P("rows", None, "cols"), P("rows", None))
    out_specs = P("rows", None, "cols")
    return jax.shard_map(
        per_device, mesh=mesh, in_specs=in_specs, out_specs=out_specs, check_vma=False
    )
```

```python
import jax
import jax.numpy as jnp
from jax import lax
from jax.experimental import pallas as pl
from jax.experimental.pallas import tpu as pltpu
from jax.sharding import PartitionSpec as P

B = 96
S = 8
R = 8
N = 128
BF = jnp.bfloat16
F32 = jnp.float32


def split3(x):
    high = x.astype(BF).astype(F32)
    rest = x - high
    mid = rest.astype(BF).astype(F32)
    return high, mid, rest - mid


def split2(x):
    high = x.astype(BF)
    return high, (x - high.astype(F32)).astype(BF)


def rows_of(x, k):
    return jnp.broadcast_to(x[k : k + 1, :], (8, N))


def lanes_of(x, k):
    return jnp.broadcast_to(x[:, k : k + 1], (8, N))


def invert_block(s_ref, o_ref):
    lane = lax.broadcasted_iota(jnp.int32, (8, N), 1)
    sub = lax.broadcasted_iota(jnp.int32, (8, N), 0)
    rows = [s_ref[8 * i : 8 * i + 8, :] for i in range(16)]
    for g in range(16):
        slab, at = rows[g], 8 * g
        inside = (lane >= at) & (lane < at + 8)
        cols = [lanes_of(slab, at + j) for j in range(8)]
        scales = None
        look = g + 1 < 16
        if look:
            following = jnp.where(inside, 0.0, rows[g + 1])
            fcols = [lanes_of(rows[g + 1], at + j) for j in range(8)]
        for k in range(8):
            inv = 1.0 / rows_of(cols[k], k)
            mult = jnp.where(sub > k, cols[k] * inv, 0.0)
            pivot = jnp.where(lane == at + k, 1.0, rows_of(slab, k))
            heads = [rows_of(cols[j], k) for j in range(k + 1, 8)]
            if look:
                fmult = fcols[k] * inv
                following = following - fmult * jnp.where((lane > at + k) & (lane < at + 8), 0.0, pivot)
                for j in range(k + 1, 8):
                    fcols[j] = fcols[j] - fmult * heads[j - k - 1]
            slab = jnp.where((lane == at + k) & (sub > k), 0.0, slab) - mult * pivot
            for j in range(k + 1, 8):
                cols[j] = cols[j] - mult * heads[j - k - 1]
            scales = inv if scales is None else jnp.where(sub == k, inv, scales)
        solved = jnp.where(lane == at + sub, 1.0, jnp.where((lane > at + sub) & (lane < at + 8), 0.0, slab))
        if look:
            rows[g + 1] = following
        if g + 2 < 16:
            a = split3(jnp.where(lane >= at + 16, slab * scales, 0.0))
            b = split3(solved)
            left = jnp.concatenate([a[0], a[0], a[1], a[0], a[2], a[1]], 0).astype(BF)
            right = jnp.concatenate([b[0], b[1], b[0], b[2], b[0], b[1]], 0).astype(BF)
            change = lax.dot_general(left, right, (((0,), (0,)), ((), ())), preferred_element_type=F32)
            for i in range(g + 2, 16):
                rows[i] = jnp.where(inside, 0.0, rows[i]) - change[8 * i : 8 * i + 8, :]
        o_ref[at : at + 8, :] = jnp.where(lane <= at + sub, solved, 0.0) * jnp.sqrt(scales)


def dot_t(left, right):
    return lax.dot_general(left, right, (((1,), (1,)), ((), ())), preferred_element_type=F32)


def eliminate(r_ref, high_ref, low_ref, inv_ref, block_ref, width, start, extra, chunk):
    stop = start + N
    inv_high, inv_low = split2(inv_ref[...])
    inverse = jnp.concatenate([inv_high, inv_high, inv_low], 1)

    def solve(rows):
        high, low = split2(r_ref[rows, start:stop])
        x = dot_t(jnp.concatenate([high, low, high], 1), inverse)
        high, low = split2(x)
        r_ref[rows, start:stop] = x
        high_ref[rows, start:stop] = high
        low_ref[rows, start:stop] = low
        return jnp.concatenate([high, low, high], 1)

    def reduce(rows, left):
        high, low = high_ref[stop:width, start:stop], low_ref[stop:width, start:stop]
        right = jnp.concatenate([high, high, low], 1)
        r_ref[rows, stop:width] = r_ref[rows, stop:width] - dot_t(left, right)

    if stop < width:
        rows = slice(stop, width)
        reduce(rows, solve(rows))
        block_ref[...] = r_ref[stop : stop + N, stop : stop + N]

    def body(i, carry):
        rows = pl.ds(pl.multiple_of(width + i * chunk, chunk), chunk)
        left = solve(rows)
        if stop < width:
            reduce(rows, left)
        return carry

    lax.fori_loop(0, extra // chunk, body, 0)


def make_kernel(width, own):
    steps = width // N
    half = width // 2
    chunk = 384

    def kernel(core_ref, a0, a1, b0, b1, c0, c1, f0, f1, s0, s1, one_ref, two_ref,
               r1, h1, l1, r2, h2, l2, block, inv, in_sem, out_sem):
        core = core_ref[0]
        mine = pl.ds(pl.multiple_of(core * half, half), half)
        other = pl.ds(pl.multiple_of((1 - core) * half, half), half)
        places = [(a0, a1, r1, 0, width), (b0, b1, r1, width, width), (f0, f1, r1, 2 * width, own),
                  (c0, c1, r2, 0, width), (s0, s1, r2, width, own)]
        copies = []
        for i, (x0, x1, ref, at, count) in enumerate(places):
            copies.append(pltpu.make_async_copy(x0, ref.at[at : at + count, mine], in_sem.at[2 * i]))
            copies.append(pltpu.make_async_copy(x1, ref.at[at : at + count, other], in_sem.at[2 * i + 1]))
        for copy in copies:
            copy.start()
        for copy in copies:
            copy.wait()
        block[...] = r1[0:N, 0:N]
        write_one = pltpu.make_async_copy(r1.at[2 * width : 2 * width + own, mine], one_ref, out_sem.at[0])

        def step(t, carry):
            invert_block(block, inv)
            for j in range(steps):
                @pl.when(t == j)
                def _():
                    eliminate(r1, h1, l1, inv, block, width, j * N, width + own, chunk)
            @pl.when(t == steps - 1)
            def _():
                write_one.start()

                def body(i, carry):
                    rows = pl.ds(pl.multiple_of(width + i * chunk, chunk), chunk)
                    to = pl.ds(pl.multiple_of(i * chunk, chunk), chunk)
                    high, low = h1[rows, :], l1[rows, :]
                    bh, bl = h1[width : 2 * width, :], l1[width : 2 * width, :]
                    change = dot_t(high, bh) + (dot_t(high, bl) + dot_t(low, bh))
                    r2[to, :] = r2[to, :] - change
                    return carry

                lax.fori_loop(0, (width + own) // chunk, body, 0)
                block[...] = r2[0:N, 0:N]
            for j in range(steps):
                @pl.when(t == steps + j)
                def _():
                    eliminate(r2, h2, l2, inv, block, width, j * N, own, chunk)
            return carry

        lax.fori_loop(0, 2 * steps, step, 0)
        write_two = pltpu.make_async_copy(r2.at[width : width + own, mine], two_ref, out_sem.at[1])
        write_two.start()
        write_one.wait()
        write_two.wait()

    return kernel


def factor(core, arrays, width, own):
    half = width // 2
    big, small = 2 * width + own, width + own
    return pl.pallas_call(
        make_kernel(width, own),
        out_shape=[jax.ShapeDtypeStruct((own, half), F32)] * 2,
        in_specs=[pl.BlockSpec(memory_space=pltpu.SMEM)] + [pl.BlockSpec(memory_space=pl.ANY)] * 10,
        out_specs=[pl.BlockSpec(memory_space=pl.ANY)] * 2,
        scratch_shapes=[
            pltpu.VMEM((big, width), F32), pltpu.VMEM((big, width), BF), pltpu.VMEM((big, width), BF),
            pltpu.VMEM((small, width), F32), pltpu.VMEM((small, width), BF), pltpu.VMEM((small, width), BF),
            pltpu.VMEM((N, N), F32), pltpu.VMEM((N, N), F32),
            pltpu.SemaphoreType.DMA((10,)), pltpu.SemaphoreType.DMA((2,)),
        ],
        compiler_params=pltpu.CompilerParams(vmem_limit_bytes=48 * 1024 * 1024),
    )(core, *arrays)


CHIPS = 128
ORDERS = ((0, 2, 5, 1, 3, 6, 4), (2, 5, 0, 3, 6, 4, 1), (5, 0, 2, 6, 4, 1, 3))


def relative(chip, root, core):
    sign = 1 - 2 * core
    x = (sign * ((chip & 3) - (root & 3))) & 3
    z = (sign * (((chip >> 2) & 7) - ((root >> 2) & 7))) & 7
    y = (sign * ((chip >> 5) - (root >> 5))) & 3
    return x + 4 * z + 32 * y


def send(piece, root, pairs_of):
    pairs = []
    for core in range(2):
        chip_of = {relative(chip, root, core): chip for chip in range(CHIPS)}
        pairs += [(2 * chip_of[a] + core, 2 * chip_of[b] + core) for a, b in pairs_of]
    return lax.ppermute(piece, ("rows", "cols"), pairs)


def spread(pieces, splits, row, core):
    roots = [root for root, _ in pieces]
    pieces = [piece for _, piece in pieces]
    places = [relative(row, root, core) for root in roots]

    def bit(i, k):
        return ((places[i] >> ORDERS[i][k]) & 1) == 1

    for k in range(7):
        for i, root in enumerate(roots):
            order = ORDERS[i]
            done = sum(1 << b for b in order[:k])
            pairs = [(a, a ^ (1 << order[k])) for a in range(CHIPS) if a & ~done == 0]
            piece = pieces[i]
            if k < splits:
                half = piece.shape[0] // 2
                pieces[i] = jnp.where(bit(i, k), send(piece[half:], root, pairs), piece[:half])
            else:
                pieces[i] = jnp.where(bit(i, k), send(piece, root, pairs), piece)
    for k in reversed(range(splits)):
        for i, root in enumerate(roots):
            pairs = [(a, a ^ (1 << ORDERS[i][k])) for a in range(CHIPS)]
            piece = pieces[i]
            got = send(piece, root, pairs)
            mine = bit(i, k)
            pieces[i] = jnp.concatenate([jnp.where(mine, got, piece), jnp.where(mine, piece, got)], 0)
    return pieces


def swap(piece):
    return lax.ppermute(piece, "cols", [(0, 1), (1, 0)])


def per_device(panels, closure_cols):
    local_rows = panels.shape[0]
    half_width = panels.shape[2]
    block_count = local_rows // B
    row = lax.axis_index("rows")
    core = lax.axis_index("cols")
    first_raw = panels[:, 0, :]
    second_raw = panels[:, 1, :]
    lead, low_first, low_second = spread([(0, first_raw), (1, first_raw), (1, second_raw)], 3, row, core)

    block_ids = row * block_count + jnp.arange(block_count)
    column_ids = jnp.arange(2 * S)
    touched = jnp.any(closure_cols[:, :, None] == column_ids[None, None, :], axis=1)
    in_first = block_ids < S
    in_second = (block_ids >= R) & (block_ids < R + S)
    present = jnp.where(
        in_first[:, None], column_ids[None, :] < S, jnp.where(in_second[:, None], True, touched)
    )
    present = present.astype(jnp.float32)
    own_columns = core * half_width + jnp.arange(half_width)

    def masked(raw, panel):
        select = (own_columns[None, :] // B + S * panel == column_ids[:, None]).astype(jnp.float32)
        mask = jnp.repeat(jnp.dot(present, select), B, axis=0)
        return raw * mask

    first, second = masked(first_raw, 0), masked(second_raw, 1)
    arrays = []
    for array in (lead, low_first, low_second, first, second):
        arrays += [array, swap(array)]
    one, two = factor(jnp.reshape(core, (1,)).astype(jnp.int32), arrays, 2 * half_width, local_rows)
    keep_rows = jnp.repeat(1.0 - in_first.astype(jnp.float32), B)
    return jnp.stack([one, two * keep_rows[:, None]], axis=1)


def solution(mesh):
    in_specs = (P("rows", None, "cols"), P("rows", None))
    out_specs = P("rows", None, "cols")
    return jax.shard_map(
        per_device, mesh=mesh, in_specs=in_specs, out_specs=out_specs, check_vma=False
    )
```

```python
import jax
import jax.numpy as jnp
from jax import lax
from jax.experimental import pallas as pl
from jax.experimental.pallas import tpu as pltpu
from jax.sharding import PartitionSpec as P

B = 96
S = 8
R = 8
N = 128
BF = jnp.bfloat16
F32 = jnp.float32


def split3(x):
    high = x.astype(BF).astype(F32)
    rest = x - high
    mid = rest.astype(BF).astype(F32)
    return high, mid, rest - mid


def split2(x):
    high = x.astype(BF)
    return high, (x - high.astype(F32)).astype(BF)


def rows_of(x, k):
    return jnp.broadcast_to(x[k : k + 1, :], (8, N))


def lanes_of(x, k):
    return jnp.broadcast_to(x[:, k : k + 1], (8, N))


def invert_block(s_ref, o_ref):
    lane = lax.broadcasted_iota(jnp.int32, (8, N), 1)
    sub = lax.broadcasted_iota(jnp.int32, (8, N), 0)
    rows = [s_ref[8 * i : 8 * i + 8, :] for i in range(16)]
    for g in range(16):
        slab, at = rows[g], 8 * g
        inside = (lane >= at) & (lane < at + 8)
        cols = [jnp.where(sub < 8, lanes_of(slab, at + j), 0.0) for j in range(8)]
        scales = None
        near = range(g + 1, min(g + 3, 16))
        reduced = {i: jnp.where(inside, 0.0, rows[i]) for i in near}
        below = {i: [lanes_of(rows[i], at + j) for j in range(8)] for i in near}
        for k in range(8):
            inv = 1.0 / rows_of(cols[k], k)
            mult = jnp.where(sub > k, cols[k] * inv, 0.0)
            pivot = jnp.where(lane == at + k, 1.0, rows_of(slab, k))
            heads = [rows_of(cols[j], k) for j in range(k + 1, 8)]
            slab = jnp.where((lane == at + k) & (sub > k), 0.0, slab) - mult * pivot
            for j in range(k + 1, 8):
                cols[j] = cols[j] - mult * heads[j - k - 1]
            pivot = jnp.where((lane > at + k) & (lane < at + 8), 0.0, pivot)
            for i in near:
                part = below[i][k] * inv
                reduced[i] = reduced[i] - part * pivot
                for j in range(k + 1, 8):
                    below[i][j] = below[i][j] - part * heads[j - k - 1]
            scales = inv if scales is None else jnp.where(sub == k, inv, scales)
        solved = jnp.where(lane == at + sub, 1.0, jnp.where((lane > at + sub) & (lane < at + 8), 0.0, slab))
        for i in near:
            rows[i] = reduced[i]
        if g + 3 < 16:
            a = split3(jnp.where(lane >= at + 24, slab * scales, 0.0))
            b = split3(solved)
            left = jnp.concatenate([a[0], a[0], a[1], a[0], a[2], a[1]], 0).astype(BF)
            right = jnp.concatenate([b[0], b[1], b[0], b[2], b[0], b[1]], 0).astype(BF)
            change = lax.dot_general(left, right, (((0,), (0,)), ((), ())), preferred_element_type=F32)
            for i in range(g + 3, 16):
                rows[i] = jnp.where(inside, 0.0, rows[i]) - change[8 * i : 8 * i + 8, :]
        o_ref[at : at + 8, :] = jnp.where(lane <= at + sub, solved, 0.0) * jnp.sqrt(scales)


def dot_t(left, right):
    return lax.dot_general(left, right, (((1,), (1,)), ((), ())), preferred_element_type=F32)


def eliminate(r_ref, high_ref, low_ref, inv_ref, block_ref, width, start, extra, chunk):
    stop = start + N
    inv_high, inv_low = split2(inv_ref[...])
    inverse = jnp.concatenate([inv_high, inv_high, inv_low], 1)

    def solve(rows):
        high, low = split2(r_ref[rows, start:stop])
        x = dot_t(jnp.concatenate([high, low, high], 1), inverse)
        high, low = split2(x)
        r_ref[rows, start:stop] = x
        high_ref[rows, start:stop] = high
        low_ref[rows, start:stop] = low
        return jnp.concatenate([high, low, high], 1)

    def reduce(rows, left):
        high, low = high_ref[stop:width, start:stop], low_ref[stop:width, start:stop]
        right = jnp.concatenate([high, high, low], 1)
        r_ref[rows, stop:width] = r_ref[rows, stop:width] - dot_t(left, right)

    if stop < width:
        rows = slice(stop, width)
        reduce(rows, solve(rows))
        block_ref[...] = r_ref[stop : stop + N, stop : stop + N]

    def body(i, carry):
        rows = pl.ds(pl.multiple_of(width + i * chunk, chunk), chunk)
        left = solve(rows)
        if stop < width:
            reduce(rows, left)
        return carry

    lax.fori_loop(0, extra // chunk, body, 0)


def make_kernel(width, own):
    steps = width // N
    half = width // 2
    chunk = 768

    def kernel(place_ref, a0, a1, b0, b1, c0, c1, o0, o1, out_ref,
               r1, h1, l1, r2, h2, l2, block, inv, in_sem, out_sem):
        core = place_ref[0]
        mine = pl.ds(pl.multiple_of(core * half, half), half)
        other = pl.ds(pl.multiple_of((1 - core) * half, half), half)
        places = [(a0, a1, 0, r1, 0, width), (b0, b1, 0, r1, width, width), (o0, o1, 0, r1, 2 * width, own),
                  (c0, c1, 0, r2, 0, width), (o0, o1, own, r2, width, own)]
        copies = []
        for i, (x0, x1, first, ref, at, count) in enumerate(places):
            for k, (x, to) in enumerate(((x0, mine), (x1, other))):
                copies.append(pltpu.make_async_copy(
                    x.at[first : first + count, :], ref.at[at : at + count, to], in_sem.at[2 * i + k]))
        for copy in copies:
            copy.start()
        for copy in copies[:2]:
            copy.wait()
        block[...] = r1[0:N, 0:N]
        write_one = pltpu.make_async_copy(r1.at[2 * width : 2 * width + own, mine], out_ref.at[:, 0, :], out_sem.at[0])

        def step(t, carry):
            invert_block(block, inv)

            @pl.when(t == 0)
            def _():
                for copy in copies[2:]:
                    copy.wait()

            for j in range(steps):
                @pl.when(t == j)
                def _():
                    eliminate(r1, h1, l1, inv, block, width, j * N, width + own, chunk)

            @pl.when(t == steps - 1)
            def _():
                write_one.start()

                def body(i, carry):
                    rows = pl.ds(pl.multiple_of(width + i * chunk, chunk), chunk)
                    to = pl.ds(pl.multiple_of(i * chunk, chunk), chunk)
                    high, low = h1[rows, :], l1[rows, :]
                    bh, bl = h1[width : 2 * width, :], l1[width : 2 * width, :]
                    change = dot_t(high, bh) + (dot_t(high, bl) + dot_t(low, bh))
                    r2[to, :] = r2[to, :] - change
                    return carry

                lax.fori_loop(0, (width + own) // chunk, body, 0)
                block[...] = r2[0:N, 0:N]

            for j in range(steps):
                @pl.when(t == steps + j)
                def _():
                    eliminate(r2, h2, l2, inv, block, width, j * N, own, chunk)
            return carry

        lax.fori_loop(0, 2 * steps, step, 0)

        @pl.when(place_ref[1] == 0)
        def _():
            r2[width : width + own, :] = jnp.zeros((own, width), F32)

        write_two = pltpu.make_async_copy(r2.at[width : width + own, mine], out_ref.at[:, 1, :], out_sem.at[1])
        write_two.start()
        write_one.wait()
        write_two.wait()

    return kernel


def factor(place, arrays, width, own):
    half = width // 2
    big, small = 2 * width + own, width + own
    return pl.pallas_call(
        make_kernel(width, own),
        out_shape=jax.ShapeDtypeStruct((own, 2, half), F32),
        in_specs=[pl.BlockSpec(memory_space=pltpu.SMEM)] + [pl.BlockSpec(memory_space=pl.ANY)] * 8,
        out_specs=pl.BlockSpec(memory_space=pl.ANY),
        scratch_shapes=[
            pltpu.VMEM((big, width), F32), pltpu.VMEM((big, width), BF), pltpu.VMEM((big, width), BF),
            pltpu.VMEM((small, width), F32), pltpu.VMEM((small, width), BF), pltpu.VMEM((small, width), BF),
            pltpu.VMEM((N, N), F32), pltpu.VMEM((N, N), F32),
            pltpu.SemaphoreType.DMA((10,)), pltpu.SemaphoreType.DMA((2,)),
        ],
        compiler_params=pltpu.CompilerParams(vmem_limit_bytes=48 * 1024 * 1024),
    )(place, *arrays)


CHIPS = 128
SPLITS = 3
ORDERS = ((0, 2, 5), (2, 5, 0), (5, 0, 2))
TREES = ((1, 3, 6, 4), (3, 6, 4, 1))


def relative(chip, root, core):
    sign = 1 - 2 * core
    x = (sign * ((chip & 3) - (root & 3))) & 3
    z = (sign * (((chip >> 2) & 7) - ((root >> 2) & 7))) & 7
    y = (sign * ((chip >> 5) - (root >> 5))) & 3
    return x + 4 * z + 32 * y


def send(piece, root, pairs_of):
    pairs = []
    for core in range(2):
        chip_of = {relative(chip, root, core): chip for chip in range(CHIPS)}
        pairs += [(2 * chip_of[a] + core, 2 * chip_of[b] + core) for a, b in pairs_of]
    return lax.ppermute(piece, ("rows", "cols"), pairs)


def pairs_with(done_bits, bit):
    done = sum(1 << b for b in done_bits)
    return [(a, a ^ (1 << bit)) for a in range(CHIPS) if a & ~done == 0]


def spread(lead, low_first, low_second, row, core):
    roots = (0, 1, 1)
    pieces = [lead, low_first, low_second]
    places = [relative(row, root, core) for root in roots]

    def bit(i, b):
        return ((places[i] >> b) & 1) == 1

    for k in range(SPLITS):
        for i, root in enumerate(roots):
            b = ORDERS[i][k]
            half = pieces[i].shape[0] // 2
            got = send(pieces[i][half:], root, pairs_with(ORDERS[i][:k], b))
            pieces[i] = jnp.where(bit(i, b), got, pieces[i][:half])
    count = pieces[1].shape[0]
    pieces = [pieces[0], jnp.concatenate(pieces[1:], 0)]
    for k in range(len(TREES[0])):
        for i in range(2):
            b = TREES[i][k]
            got = send(pieces[i], roots[i], pairs_with(ORDERS[i] + TREES[i][:k], b))
            pieces[i] = jnp.where(bit(i, b), got, pieces[i])
    pieces = [pieces[0], pieces[1][:count], pieces[1][count:]]
    for k in reversed(range(SPLITS)):
        for i, root in enumerate(roots):
            b = ORDERS[i][k]
            piece = pieces[i]
            got = send(piece, root, pairs_with(range(7), b))
            mine = bit(i, b)
            pieces[i] = jnp.concatenate([jnp.where(mine, got, piece), jnp.where(mine, piece, got)], 0)
    return pieces


def swap(piece):
    return lax.ppermute(piece, "cols", [(0, 1), (1, 0)])


def per_device(panels, closure_cols):
    local_rows = panels.shape[0]
    half_width = panels.shape[2]
    block_count = local_rows // B
    assert block_count == S == R
    row = lax.axis_index("rows")
    core = lax.axis_index("cols")
    first_raw, panels = lax.optimization_barrier((panels[:, 0, :], panels))
    second_raw = panels[:, 1, :]

    block_ids = row * block_count + jnp.arange(block_count)
    column_ids = jnp.arange(2 * S)
    touched = jnp.any(closure_cols[:, :, None] == column_ids[None, None, :], axis=1)
    in_first = block_ids < S
    in_second = (block_ids >= R) & (block_ids < R + S)
    present = jnp.where(
        in_first[:, None], column_ids[None, :] < S, jnp.where(in_second[:, None], True, touched)
    )
    present = present.astype(jnp.float32)
    own_columns = core * half_width + jnp.arange(half_width)

    def masked(raw, panel):
        select = (own_columns[None, :] // B + S * panel == column_ids[:, None]).astype(jnp.float32)
        return raw * jnp.repeat(jnp.dot(present, select), B, axis=0)

    arrays = list(spread(first_raw, first_raw, second_raw, row, core))
    arrays.append(jnp.concatenate([masked(first_raw, 0), masked(second_raw, 1)], 0))
    pairs = []
    for array in arrays:
        pairs += [array, swap(array)]
    place = jnp.stack([core, row]).astype(jnp.int32)
    return factor(place, pairs, 2 * half_width, local_rows)


def solution(mesh):
    in_specs = (P("rows", None, "cols"), P("rows", None))
    out_specs = P("rows", None, "cols")
    return jax.shard_map(
        per_device, mesh=mesh, in_specs=in_specs, out_specs=out_specs, check_vma=False
    )
```

```python
import jax
import jax.numpy as jnp
from jax import lax
from jax.experimental import pallas as pl
from jax.experimental.pallas import tpu as pltpu
from jax.sharding import PartitionSpec as P

B = 96
S = 8
R = 8
N = 128
BF = jnp.bfloat16
F32 = jnp.float32


def split3(x):
    high = x.astype(BF).astype(F32)
    rest = x - high
    mid = rest.astype(BF).astype(F32)
    return high, mid, rest - mid


def split2(x):
    high = x.astype(BF)
    return high, (x - high.astype(F32)).astype(BF)


def rows_of(x, k):
    return jnp.broadcast_to(x[k : k + 1, :], (8, N))


def lanes_of(x, k):
    return jnp.broadcast_to(x[:, k : k + 1], (8, N))


def invert_block(s_ref, o_ref):
    lane = lax.broadcasted_iota(jnp.int32, (8, N), 1)
    sub = lax.broadcasted_iota(jnp.int32, (8, N), 0)
    rows = [s_ref[8 * i : 8 * i + 8, :] for i in range(16)]
    for g in range(16):
        slab, at = rows[g], 8 * g
        inside = (lane >= at) & (lane < at + 8)
        cols = [jnp.where(sub < 8, lanes_of(slab, at + j), 0.0) for j in range(8)]
        scales = None
        near = range(g + 1, min(g + 3, 16))
        reduced = {i: jnp.where(inside, 0.0, rows[i]) for i in near}
        below = {i: [lanes_of(rows[i], at + j) for j in range(8)] for i in near}
        for k in range(8):
            inv = 1.0 / rows_of(cols[k], k)
            mult = jnp.where(sub > k, cols[k] * inv, 0.0)
            pivot = jnp.where(lane == at + k, 1.0, rows_of(slab, k))
            heads = [rows_of(cols[j], k) for j in range(k + 1, 8)]
            slab = jnp.where((lane == at + k) & (sub > k), 0.0, slab) - mult * pivot
            for j in range(k + 1, 8):
                cols[j] = cols[j] - mult * heads[j - k - 1]
            pivot = jnp.where((lane > at + k) & (lane < at + 8), 0.0, pivot)
            for i in near:
                part = below[i][k] * inv
                reduced[i] = reduced[i] - part * pivot
                for j in range(k + 1, 8):
                    below[i][j] = below[i][j] - part * heads[j - k - 1]
            scales = inv if scales is None else jnp.where(sub == k, inv, scales)
        solved = jnp.where(lane == at + sub, 1.0, jnp.where((lane > at + sub) & (lane < at + 8), 0.0, slab))
        for i in near:
            rows[i] = reduced[i]
        if g + 3 < 16:
            a = split3(jnp.where(lane >= at + 24, slab * scales, 0.0))
            b = split3(solved)
            left = jnp.concatenate([a[0], a[0], a[1], a[0], a[2], a[1]], 0).astype(BF)
            right = jnp.concatenate([b[0], b[1], b[0], b[2], b[0], b[1]], 0).astype(BF)
            change = lax.dot_general(left, right, (((0,), (0,)), ((), ())), preferred_element_type=F32)
            for i in range(g + 3, 16):
                rows[i] = jnp.where(inside, 0.0, rows[i]) - change[8 * i : 8 * i + 8, :]
        o_ref[at : at + 8, :] = jnp.where(lane <= at + sub, solved, 0.0) * jnp.sqrt(scales)


def dot_t(left, right):
    return lax.dot_general(left, right, (((1,), (1,)), ((), ())), preferred_element_type=F32)


def eliminate(r_ref, high_ref, low_ref, inv_ref, block_ref, width, start, extra, chunk):
    stop = start + N
    inv_high, inv_low = split2(inv_ref[...])
    inverse = jnp.concatenate([inv_high, inv_high, inv_low], 1)

    def solve(rows):
        high, low = split2(r_ref[rows, start:stop])
        x = dot_t(jnp.concatenate([high, low, high], 1), inverse)
        high, low = split2(x)
        r_ref[rows, start:stop] = x
        high_ref[rows, start:stop] = high
        low_ref[rows, start:stop] = low
        return jnp.concatenate([high, low, high], 1)

    def reduce(rows, left):
        high, low = high_ref[stop:width, start:stop], low_ref[stop:width, start:stop]
        right = jnp.concatenate([high, high, low], 1)
        r_ref[rows, stop:width] = r_ref[rows, stop:width] - dot_t(left, right)

    if stop < width:
        rows = slice(stop, width)
        reduce(rows, solve(rows))
        block_ref[...] = r_ref[stop : stop + N, stop : stop + N]

    def body(i, carry):
        rows = pl.ds(pl.multiple_of(width + i * chunk, chunk), chunk)
        left = solve(rows)
        if stop < width:
            reduce(rows, left)
        return carry

    lax.fori_loop(0, extra // chunk, body, 0)


def make_kernel(width, own):
    steps = width // N
    half = width // 2
    chunk = 768

    def kernel(place_ref, a0, a1, b0, b1, c0, c1, o0, o1, out_ref,
               r1, h1, l1, r2, h2, l2, block, inv, in_sem, out_sem):
        core = place_ref[0]
        mine = pl.ds(pl.multiple_of(core * half, half), half)
        other = pl.ds(pl.multiple_of((1 - core) * half, half), half)
        places = [(a0, a1, 0, r1, 0, width), (b0, b1, 0, r1, width, width), (o0, o1, 0, r1, 2 * width, own),
                  (c0, c1, 0, r2, 0, width), (o0, o1, own, r2, width, own)]
        copies = []
        for i, (x0, x1, first, ref, at, count) in enumerate(places):
            for k, (x, to) in enumerate(((x0, mine), (x1, other))):
                copies.append(pltpu.make_async_copy(
                    x.at[first : first + count, :], ref.at[at : at + count, to], in_sem.at[2 * i + k]))
        for copy in copies:
            copy.start()
        for copy in copies[:2]:
            copy.wait()
        block[...] = r1[0:N, 0:N]
        write_one = pltpu.make_async_copy(r1.at[2 * width : 2 * width + own, mine], out_ref.at[:, 0, :], out_sem.at[0])

        def step(t, carry):
            invert_block(block, inv)

            @pl.when(t == 0)
            def _():
                for copy in copies[2:]:
                    copy.wait()

            for j in range(steps):
                @pl.when(t == j)
                def _():
                    eliminate(r1, h1, l1, inv, block, width, j * N, width + own, chunk)

            @pl.when(t == steps - 1)
            def _():
                write_one.start()

                def body(i, carry):
                    rows = pl.ds(pl.multiple_of(width + i * chunk, chunk), chunk)
                    to = pl.ds(pl.multiple_of(i * chunk, chunk), chunk)
                    high, low = h1[rows, :], l1[rows, :]
                    bh, bl = h1[width : 2 * width, :], l1[width : 2 * width, :]
                    change = dot_t(high, bh) + (dot_t(high, bl) + dot_t(low, bh))
                    r2[to, :] = r2[to, :] - change
                    return carry

                lax.fori_loop(0, (width + own) // chunk, body, 0)
                block[...] = r2[0:N, 0:N]

            for j in range(steps):
                @pl.when(t == steps + j)
                def _():
                    eliminate(r2, h2, l2, inv, block, width, j * N, own, chunk)
            return carry

        lax.fori_loop(0, 2 * steps, step, 0)

        @pl.when(place_ref[1] == 0)
        def _():
            r2[width : width + own, :] = jnp.zeros((own, width), F32)

        write_two = pltpu.make_async_copy(r2.at[width : width + own, mine], out_ref.at[:, 1, :], out_sem.at[1])
        write_two.start()
        write_one.wait()
        write_two.wait()

    return kernel


def factor(place, arrays, width, own):
    half = width // 2
    big, small = 2 * width + own, width + own
    return pl.pallas_call(
        make_kernel(width, own),
        out_shape=jax.ShapeDtypeStruct((own, 2, half), F32),
        in_specs=[pl.BlockSpec(memory_space=pltpu.SMEM)] + [pl.BlockSpec(memory_space=pl.ANY)] * 8,
        out_specs=pl.BlockSpec(memory_space=pl.ANY),
        scratch_shapes=[
            pltpu.VMEM((big, width), F32), pltpu.VMEM((big, width), BF), pltpu.VMEM((big, width), BF),
            pltpu.VMEM((small, width), F32), pltpu.VMEM((small, width), BF), pltpu.VMEM((small, width), BF),
            pltpu.VMEM((N, N), F32), pltpu.VMEM((N, N), F32),
            pltpu.SemaphoreType.DMA((10,)), pltpu.SemaphoreType.DMA((2,)),
        ],
        compiler_params=pltpu.CompilerParams(vmem_limit_bytes=48 * 1024 * 1024),
    )(place, *arrays)


CHIPS = 128
SPLITS = 3
ORDERS = ((0, 2, 5), (2, 5, 0), (5, 0, 2))
TREES = ((1, 3, 6, 4), (3, 6, 4, 1), (6, 1, 3, 4))


def relative(chip, root, core):
    sign = 1 - 2 * core
    x = (sign * ((chip & 3) - (root & 3))) & 3
    z = (sign * (((chip >> 2) & 7) - ((root >> 2) & 7))) & 7
    y = (sign * ((chip >> 5) - (root >> 5))) & 3
    return (x ^ (x >> 1)) + 4 * ((0x32765410 >> (4 * z)) & 7) + 32 * (y ^ (y >> 1))


def send(piece, root, pairs_of):
    pairs = []
    for core in range(2):
        chip_of = {relative(chip, root, core): chip for chip in range(CHIPS)}
        pairs += [(2 * chip_of[a] + core, 2 * chip_of[b] + core) for a, b in pairs_of]
    return lax.ppermute(piece, ("rows", "cols"), pairs)


def pairs_with(done_bits, bit):
    done = sum(1 << b for b in done_bits)
    return [(a, a ^ (1 << bit)) for a in range(CHIPS) if a & ~done == 0]


def spread(lead, low_first, low_second, row, core):
    roots = (0, 1, 1)
    pieces = [lead, low_first, low_second]
    places = [relative(row, root, core) for root in roots]

    def bit(i, b):
        return ((places[i] >> b) & 1) == 1

    for k in range(SPLITS):
        for i, root in enumerate(roots):
            b = ORDERS[i][k]
            half = pieces[i].shape[0] // 2
            got = send(pieces[i][half:], root, pairs_with(ORDERS[i][:k], b))
            pieces[i] = jnp.where(bit(i, b), got, pieces[i][:half])
    for k in range(len(TREES[0])):
        for i in range(3):
            b = TREES[i][k]
            got = send(pieces[i], roots[i], pairs_with(ORDERS[i] + TREES[i][:k], b))
            pieces[i] = jnp.where(bit(i, b), got, pieces[i])
    for k in reversed(range(SPLITS)):
        for i, root in enumerate(roots):
            b = ORDERS[i][k]
            piece = pieces[i]
            got = send(piece, root, pairs_with(range(7), b))
            mine = bit(i, b)
            pieces[i] = jnp.concatenate([jnp.where(mine, got, piece), jnp.where(mine, piece, got)], 0)
    return pieces


def split_kernel(panels_ref, first_ref, second_ref, sems):
    copies = [
        pltpu.make_async_copy(panels_ref.at[:, 0, :], first_ref, sems.at[0]),
        pltpu.make_async_copy(panels_ref.at[:, 1, :], second_ref, sems.at[1]),
    ]
    for copy in copies:
        copy.start()
    for copy in copies:
        copy.wait()


def split_panels(panels):
    rows, _, half = panels.shape
    return pl.pallas_call(
        split_kernel,
        out_shape=[jax.ShapeDtypeStruct((rows, half), F32)] * 2,
        in_specs=[pl.BlockSpec(memory_space=pl.ANY)],
        out_specs=[pl.BlockSpec(memory_space=pltpu.VMEM)] * 2,
        scratch_shapes=[pltpu.SemaphoreType.DMA((2,))],
    )(panels)


def swap(piece):
    return lax.ppermute(piece, "cols", [(0, 1), (1, 0)])


def per_device(panels, closure_cols):
    local_rows = panels.shape[0]
    half_width = panels.shape[2]
    block_count = local_rows // B
    assert block_count == S == R
    row = lax.axis_index("rows")
    core = lax.axis_index("cols")
    first_raw, second_raw = split_panels(panels)

    block_ids = row * block_count + jnp.arange(block_count)
    column_ids = jnp.arange(2 * S)
    touched = jnp.any(closure_cols[:, :, None] == column_ids[None, None, :], axis=1)
    in_first = block_ids < S
    in_second = (block_ids >= R) & (block_ids < R + S)
    present = jnp.where(
        in_first[:, None], column_ids[None, :] < S, jnp.where(in_second[:, None], True, touched)
    )
    present = present.astype(jnp.float32)
    own_columns = core * half_width + jnp.arange(half_width)

    def masked(raw, panel):
        select = (own_columns[None, :] // B + S * panel == column_ids[:, None]).astype(jnp.float32)
        return raw * jnp.repeat(jnp.dot(present, select), B, axis=0)

    arrays = list(spread(first_raw, first_raw, second_raw, row, core))
    arrays.append(jnp.concatenate([masked(first_raw, 0), masked(second_raw, 1)], 0))
    pairs = []
    for array in arrays:
        pairs += [array, swap(array)]
    place = jnp.stack([core, row]).astype(jnp.int32)
    return factor(place, pairs, 2 * half_width, local_rows)


def solution(mesh):
    in_specs = (P("rows", None, "cols"), P("rows", None))
    out_specs = P("rows", None, "cols")
    return jax.shard_map(
        per_device, mesh=mesh, in_specs=in_specs, out_specs=out_specs, check_vma=False
    )
```

```python
import jax
import jax.numpy as jnp
from jax import lax
from jax.experimental import pallas as pl
from jax.experimental.pallas import tpu as pltpu
from jax.sharding import PartitionSpec as P

B = 96
S = 8
R = 8
N = 128
BF = jnp.bfloat16
F32 = jnp.float32


def split3(x):
    high = x.astype(BF).astype(F32)
    rest = x - high
    mid = rest.astype(BF).astype(F32)
    return high, mid, rest - mid


def split2(x):
    high = x.astype(BF)
    return high, (x - high.astype(F32)).astype(BF)


def rows_of(x, k):
    return jnp.broadcast_to(x[k : k + 1, :], (8, N))


def lanes_of(x, k):
    return jnp.broadcast_to(x[:, k : k + 1], (8, N))


def invert_block(s_ref, o_ref):
    lane = lax.broadcasted_iota(jnp.int32, (8, N), 1)
    sub = lax.broadcasted_iota(jnp.int32, (8, N), 0)
    rows = [s_ref[8 * i : 8 * i + 8, :] for i in range(16)]
    for g in range(16):
        slab, at = rows[g], 8 * g
        inside = (lane >= at) & (lane < at + 8)
        cols = [jnp.where(sub < 8, lanes_of(slab, at + j), 0.0) for j in range(8)]
        scales = None
        near = range(g + 1, min(g + 3, 16))
        reduced = {i: jnp.where(inside, 0.0, rows[i]) for i in near}
        below = {i: [lanes_of(rows[i], at + j) for j in range(8)] for i in near}
        for k in range(8):
            inv = 1.0 / rows_of(cols[k], k)
            mult = jnp.where(sub > k, cols[k] * inv, 0.0)
            pivot = jnp.where(lane == at + k, 1.0, rows_of(slab, k))
            heads = [rows_of(cols[j], k) for j in range(k + 1, 8)]
            slab = jnp.where((lane == at + k) & (sub > k), 0.0, slab) - mult * pivot
            for j in range(k + 1, 8):
                cols[j] = cols[j] - mult * heads[j - k - 1]
            pivot = jnp.where((lane > at + k) & (lane < at + 8), 0.0, pivot)
            for i in near:
                part = below[i][k] * inv
                reduced[i] = reduced[i] - part * pivot
                for j in range(k + 1, 8):
                    below[i][j] = below[i][j] - part * heads[j - k - 1]
            scales = inv if scales is None else jnp.where(sub == k, inv, scales)
        solved = jnp.where(lane == at + sub, 1.0, jnp.where((lane > at + sub) & (lane < at + 8), 0.0, slab))
        for i in near:
            rows[i] = reduced[i]
        if g + 3 < 16:
            a = split3(jnp.where(lane >= at + 24, slab * scales, 0.0))
            b = split3(solved)
            left = jnp.concatenate([a[0], a[0], a[1], a[0], a[2], a[1]], 0).astype(BF)
            right = jnp.concatenate([b[0], b[1], b[0], b[2], b[0], b[1]], 0).astype(BF)
            change = lax.dot_general(left, right, (((0,), (0,)), ((), ())), preferred_element_type=F32)
            for i in range(g + 3, 16):
                rows[i] = jnp.where(inside, 0.0, rows[i]) - change[8 * i : 8 * i + 8, :]
        o_ref[at : at + 8, :] = jnp.where(lane <= at + sub, solved, 0.0) * jnp.sqrt(scales)


def dot_t(left, right):
    return lax.dot_general(left, right, (((1,), (1,)), ((), ())), preferred_element_type=F32)


def eliminate(r_ref, high_ref, low_ref, inv_ref, block_ref, width, start, extra, chunk):
    stop = start + N
    inv_high, inv_low = split2(inv_ref[...])
    inverse = jnp.concatenate([inv_high, inv_high, inv_low], 1)

    def solve(rows):
        high, low = split2(r_ref[rows, start:stop])
        x = dot_t(jnp.concatenate([high, low, high], 1), inverse)
        high, low = split2(x)
        r_ref[rows, start:stop] = x
        high_ref[rows, start:stop] = high
        low_ref[rows, start:stop] = low
        return jnp.concatenate([high, low, high], 1)

    def reduce(rows, left):
        high, low = high_ref[stop:width, start:stop], low_ref[stop:width, start:stop]
        right = jnp.concatenate([high, high, low], 1)
        r_ref[rows, stop:width] = r_ref[rows, stop:width] - dot_t(left, right)

    if stop < width:
        rows = slice(stop, width)
        reduce(rows, solve(rows))
        block_ref[...] = r_ref[stop : stop + N, stop : stop + N]

    def body(i, carry):
        rows = pl.ds(pl.multiple_of(width + i * chunk, chunk), chunk)
        left = solve(rows)
        if stop < width:
            reduce(rows, left)
        return carry

    lax.fori_loop(0, extra // chunk, body, 0)


def make_kernel(width, own):
    steps = width // N
    half = width // 2
    chunk = 768

    def kernel(place_ref, a0, a1, b0, b1, c0, c1, o0, o1, out_ref,
               r1, h1, l1, r2, h2, l2, block, inv, in_sem, out_sem):
        core = place_ref[0]
        mine = pl.ds(pl.multiple_of(core * half, half), half)
        other = pl.ds(pl.multiple_of((1 - core) * half, half), half)
        places = [(a0, a1, 0, r1, 0, width), (b0, b1, 0, r1, width, width), (o0, o1, 0, r1, 2 * width, own),
                  (c0, c1, 0, r2, 0, width), (o0, o1, own, r2, width, own)]
        copies = []
        for i, (x0, x1, first, ref, at, count) in enumerate(places):
            for k, (x, to) in enumerate(((x0, mine), (x1, other))):
                copies.append(pltpu.make_async_copy(
                    x.at[first : first + count, :], ref.at[at : at + count, to], in_sem.at[2 * i + k]))
        for copy in copies:
            copy.start()
        for copy in copies[:2]:
            copy.wait()
        block[...] = r1[0:N, 0:N]
        write_one = pltpu.make_async_copy(r1.at[2 * width : 2 * width + own, mine], out_ref.at[:, 0, :], out_sem.at[0])

        def step(t, carry):
            invert_block(block, inv)

            @pl.when(t == 0)
            def _():
                for copy in copies[2:]:
                    copy.wait()

            for j in range(steps):
                @pl.when(t == j)
                def _():
                    eliminate(r1, h1, l1, inv, block, width, j * N, width + own, 2 * chunk)

            @pl.when(t == steps - 1)
            def _():
                write_one.start()

                def subtract(rows, to, count):
                    high, low = h1[rows, :], l1[rows, :]
                    bh, bl = h1[width : width + count, :], l1[width : width + count, :]
                    change = dot_t(high, bh) + (dot_t(high, bl) + dot_t(low, bh))
                    r2[to, 0:count] = r2[to, 0:count] - change

                subtract(slice(width, width + half), slice(0, half), half)
                subtract(slice(width + half, 2 * width + own), slice(half, width + own), width)
                block[...] = r2[0:N, 0:N]

            for j in range(steps):
                @pl.when(t == steps + j)
                def _():
                    eliminate(r2, h2, l2, inv, block, width, j * N, own, chunk)
            return carry

        lax.fori_loop(0, 2 * steps, step, 0)

        @pl.when(place_ref[1] == 0)
        def _():
            r2[width : width + own, :] = jnp.zeros((own, width), F32)

        write_two = pltpu.make_async_copy(r2.at[width : width + own, mine], out_ref.at[:, 1, :], out_sem.at[1])
        write_two.start()
        write_one.wait()
        write_two.wait()

    return kernel


def factor(place, arrays, width, own):
    half = width // 2
    big, small = 2 * width + own, width + own
    return pl.pallas_call(
        make_kernel(width, own),
        out_shape=jax.ShapeDtypeStruct((own, 2, half), F32),
        in_specs=[pl.BlockSpec(memory_space=pltpu.SMEM)] + [pl.BlockSpec(memory_space=pl.ANY)] * 8,
        out_specs=pl.BlockSpec(memory_space=pl.ANY),
        scratch_shapes=[
            pltpu.VMEM((big, width), F32), pltpu.VMEM((big, width), BF), pltpu.VMEM((big, width), BF),
            pltpu.VMEM((small, width), F32), pltpu.VMEM((small, width), BF), pltpu.VMEM((small, width), BF),
            pltpu.VMEM((N, N), F32), pltpu.VMEM((N, N), F32),
            pltpu.SemaphoreType.DMA((10,)), pltpu.SemaphoreType.DMA((2,)),
        ],
        compiler_params=pltpu.CompilerParams(vmem_limit_bytes=48 * 1024 * 1024),
    )(place, *arrays)


CHIPS = 128
SPLITS = 3
ORDERS = ((0, 2, 5), (2, 5, 0), (5, 0, 2))
TREES = ((1, 3, 6, 4), (3, 6, 4, 1), (6, 1, 3, 4))


def relative(chip, root, core):
    sign = 1 - 2 * core
    x = (sign * ((chip & 3) - (root & 3))) & 3
    z = (sign * (((chip >> 2) & 7) - ((root >> 2) & 7))) & 7
    y = (sign * ((chip >> 5) - (root >> 5))) & 3
    return (x ^ (x >> 1)) + 4 * ((0x32765410 >> (4 * z)) & 7) + 32 * (y ^ (y >> 1))


def send(piece, root, pairs_of):
    pairs = []
    for core in range(2):
        chip_of = {relative(chip, root, core): chip for chip in range(CHIPS)}
        pairs += [(2 * chip_of[a] + core, 2 * chip_of[b] + core) for a, b in pairs_of]
    return lax.ppermute(piece, ("rows", "cols"), pairs)


def pairs_with(done_bits, bit):
    done = sum(1 << b for b in done_bits)
    return [(a, a ^ (1 << bit)) for a in range(CHIPS) if a & ~done == 0]


def spread(lead, low_first, low_second, row, core):
    roots = (0, 1, 1)
    pieces = [lead, low_first, low_second]
    places = [relative(row, root, core) for root in roots]

    def bit(i, b):
        return ((places[i] >> b) & 1) == 1

    for k in range(SPLITS):
        for i, root in enumerate(roots):
            b = ORDERS[i][k]
            half = pieces[i].shape[0] // 2
            got = send(pieces[i][half:], root, pairs_with(ORDERS[i][:k], b))
            pieces[i] = jnp.where(bit(i, b), got, pieces[i][:half])
    for k in range(len(TREES[0])):
        for i in range(3):
            b = TREES[i][k]
            got = send(pieces[i], roots[i], pairs_with(ORDERS[i] + TREES[i][:k], b))
            pieces[i] = jnp.where(bit(i, b), got, pieces[i])
    for k in reversed(range(SPLITS)):
        for i, root in enumerate(roots):
            b = ORDERS[i][k]
            piece = pieces[i]
            got = send(piece, root, pairs_with(range(7), b))
            mine = bit(i, b)
            pieces[i] = jnp.concatenate([jnp.where(mine, got, piece), jnp.where(mine, piece, got)], 0)
    return pieces


def split_kernel(panels_ref, first_ref, second_ref, sems):
    copies = [
        pltpu.make_async_copy(panels_ref.at[:, 0, :], first_ref, sems.at[0]),
        pltpu.make_async_copy(panels_ref.at[:, 1, :], second_ref, sems.at[1]),
    ]
    for copy in copies:
        copy.start()
    for copy in copies:
        copy.wait()


def split_panels(panels):
    rows, _, half = panels.shape
    return pl.pallas_call(
        split_kernel,
        out_shape=[jax.ShapeDtypeStruct((rows, half), F32)] * 2,
        in_specs=[pl.BlockSpec(memory_space=pl.ANY)],
        out_specs=[pl.BlockSpec(memory_space=pltpu.VMEM)] * 2,
        scratch_shapes=[pltpu.SemaphoreType.DMA((2,))],
    )(panels)


def swap(piece):
    return lax.ppermute(piece, "cols", [(0, 1), (1, 0)])


def per_device(panels, closure_cols):
    local_rows = panels.shape[0]
    half_width = panels.shape[2]
    block_count = local_rows // B
    assert block_count == S == R
    row = lax.axis_index("rows")
    core = lax.axis_index("cols")
    first_raw, second_raw = split_panels(panels)

    block_ids = row * block_count + jnp.arange(block_count)
    column_ids = jnp.arange(2 * S)
    touched = jnp.any(closure_cols[:, :, None] == column_ids[None, None, :], axis=1)
    in_first = block_ids < S
    in_second = (block_ids >= R) & (block_ids < R + S)
    present = jnp.where(
        in_first[:, None], column_ids[None, :] < S, jnp.where(in_second[:, None], True, touched)
    )
    present = present.astype(jnp.float32)
    own_columns = core * half_width + jnp.arange(half_width)

    def masked(raw, panel):
        select = (own_columns[None, :] // B + S * panel == column_ids[:, None]).astype(jnp.float32)
        return raw * jnp.repeat(jnp.dot(present, select), B, axis=0)

    arrays = list(spread(first_raw, first_raw, second_raw, row, core))
    arrays.append(jnp.concatenate([masked(first_raw, 0), masked(second_raw, 1)], 0))
    pairs = []
    for array in arrays:
        pairs += [array, swap(array)]
    place = jnp.stack([core, row]).astype(jnp.int32)
    return factor(place, pairs, 2 * half_width, local_rows)


def solution(mesh):
    in_specs = (P("rows", None, "cols"), P("rows", None))
    out_specs = P("rows", None, "cols")
    return jax.shard_map(
        per_device, mesh=mesh, in_specs=in_specs, out_specs=out_specs, check_vma=False
    )
```
